32 devices in a mesh: dp: 4 (over x, core), mp: 8 (over z, y).
Axes of the slice: x: 2, y: 2, z: 4, core: 2. Of those that a mesh axis runs over, the one named last changes fastest.
Arguments:
- partial_grads: bfloat16 [4, 48, 512, 512], P('dp', None, 'mp'), may hold values from -5 to 5
- owner_device: int32 [48], replicated, may hold values from 0 to 31, as said below
- layer_of: int32 [48], replicated, may hold values from 0 to 3
- stat_left: float32 [64, 512, 512], P(('dp', 'mp')), as said below
- stat_right: float32 [64, 512, 512], P(('dp', 'mp')), as said below
- basis_left: float32 [64, 512, 512], P(('dp', 'mp'))
- basis_right: float32 [64, 512, 512], P(('dp', 'mp'))
- moment_first: float32 [64, 512, 512], P(('dp', 'mp')), may hold values from -4 to 4
- moment_second: float32 [64, 512, 512], P(('dp', 'mp')), may hold values from 0.02 to 2
Outputs:
- update: bfloat16 [48, 512, 512], P('dp', 'mp')
- stat_left_next: float32 [64, 512, 512], P(('dp', 'mp'))
- stat_right_next: float32 [64, 512, 512], P(('dp', 'mp'))
- basis_left_next: float32 [64, 512, 512], P(('dp', 'mp'))
- basis_right_next: float32 [64, 512, 512], P(('dp', 'mp'))
- moment_first_next: float32 [64, 512, 512], P(('dp', 'mp'))
- moment_second_next: float32 [64, 512, 512], P(('dp', 'mp'))
The draws below stay inside these ranges and needn't reach their ends.
Inputs may be any that keep to these rules, and one draw needn't show every extreme that they name: `owner_device`: no device index is named by more than 2 blocks, and some device is named by exactly 2. `stat_left`: every slot's matrix is symmetric. `stat_right`: every slot's matrix is symmetric.
All inputs are finite; a program needn't handle non-finite values.
Results may differ from the reference program's by a relative error of at most 0.001.
Values may be sent and summed in bfloat16 or wider, within the bound.
No kernel may reach another device: no remote copies, remote signals or barrier semaphores. Data moves between devices by JAX's collectives and lax.ppermute only.
A program may use at most 128 MiB of HBM per device.

```python
import math
import jax
import jax.numpy as jnp
from jax import lax

D = 512
CAPD = 2
ITERS = 4
LAYERS = 4
BLOCKS = 48
SLOTS = 64
N_DP = 4
DEVICES = 32


def draw_owner_device(key, part):
    first_key, second_key, third_key = jax.random.split(jax.random.fold_in(key, 11), 3)
    shuffled = jax.random.permutation(first_key, DEVICES)
    upper_full = BLOCKS // CAPD
    spare = max(1, CAPD - 1)
    needed = -(-(BLOCKS - DEVICES) // spare)
    lower_full = max(1, min(max(BLOCKS // 4, needed), upper_full))
    full_count = jax.random.randint(second_key, (), lower_full, upper_full + 1)
    position = jnp.arange(BLOCKS)
    chosen = jnp.where(position < CAPD * full_count, position // CAPD, full_count + position - CAPD * full_count)
    owners = shuffled[chosen]
    return owners[jax.random.permutation(third_key, BLOCKS)].astype(jnp.int32)


def statistic(key):
    diag_key, noise_key = jax.random.split(key)
    diagonal = jnp.exp(jax.random.uniform(diag_key, (SLOTS, D), jnp.float32, math.log(D / 4.0), math.log(2.0 * D)))
    noise = jax.random.normal(noise_key, (SLOTS, D, D), jnp.float32) * (1.4 * math.sqrt(D))
    symmetric = noise + jnp.swapaxes(noise, 1, 2)
    return symmetric + diagonal[:, :, None] * jnp.eye(D, dtype=jnp.float32)[None]


def basis_draw(key):
    noise = jax.random.normal(key, (SLOTS, D, D), jnp.float32) * (0.6 / math.sqrt(D))
    return noise + jnp.eye(D, dtype=jnp.float32)[None]


def draw_stat_left(key, part):
    return statistic(jax.random.fold_in(key, 21))


def draw_stat_right(key, part):
    return statistic(jax.random.fold_in(key, 22))


def draw_basis_left(key, part):
    return basis_draw(jax.random.fold_in(key, 31))


def draw_basis_right(key, part):
    return basis_draw(jax.random.fold_in(key, 32))


def place_ends(values, rng, smallest, largest):
    index_at = [jax.random.randint(jax.random.fold_in(rng, axis), (), 0, length) for axis, length in enumerate(values.shape)]
    longest = values.shape.index(max(values.shape))
    beside = index_at[:longest] + [(index_at[longest] + 1) % values.shape[longest]] + index_at[longest + 1:]
    return values.at[tuple(index_at)].set(smallest).at[tuple(beside)].set(largest)


def steps_of(rng, shape, pieces, least, top_value):
    loudness = 1.0
    for axis_at, blocks in pieces:
        heights = jax.random.uniform(jax.random.fold_in(jax.random.fold_in(rng, 6), axis_at), (blocks,), jnp.float32, least / len(pieces), top_value / len(pieces))
        loudness = loudness * jnp.repeat(jnp.exp(heights), shape[axis_at] // blocks).reshape((-1,) + (1,) * (len(shape) - 1 - axis_at))
    return loudness


def gaussian(key, shape, width, most, cuts=(), kind=jnp.bfloat16):
    gain = steps_of(key, shape, cuts, -0.22, 0.18) if cuts else 1.0
    drawn = jax.random.normal(key, shape, jnp.float32) * width * gain
    return jnp.minimum(jnp.maximum(drawn, -most), most).astype(kind)


def setup_inputs(seed: int = 0) -> dict:
    seeds = jax.random.split(jax.random.key(seed), 10)
    partial_grads = gaussian(seeds[0], (N_DP, BLOCKS, D, D), 0.35, 5.0, ((0, 4), (2, 8)))
    owner_device = draw_owner_device(jax.random.fold_in(seeds[9], 71), 0)
    layer_of = place_ends(jax.random.randint(seeds[2], (BLOCKS,), 0, LAYERS), jax.random.fold_in(seeds[2], 1), 0, LAYERS - 1).astype(jnp.int32)
    stat_left = draw_stat_left(jax.random.fold_in(seeds[9], 71), 0)
    stat_right = draw_stat_right(jax.random.fold_in(seeds[9], 71), 0)
    basis_left = draw_basis_left(jax.random.fold_in(seeds[9], 71), 0)
    basis_right = draw_basis_right(jax.random.fold_in(seeds[9], 71), 0)
    moment_first = gaussian(seeds[7], (SLOTS, D, D), 0.5, 4.0, ((0, 32),), jnp.float32)
    moment_second = jnp.clip(jnp.exp(math.log(2.0) - 4.6051702 * jax.random.uniform(seeds[8], (SLOTS, D, D), jnp.float32) ** steps_of(seeds[8], (SLOTS, D, D), ((0, 32),), -0.2, 0.2)), 0.02, 2.0)
    return dict(partial_grads=partial_grads, owner_device=owner_device, layer_of=layer_of, stat_left=stat_left, stat_right=stat_right, basis_left=basis_left, basis_right=basis_right, moment_first=moment_first, moment_second=moment_second)


PRECISE = lax.Precision.HIGHEST
BETA_ONE = 0.9
BETA_TWO = 0.95
SHRINK = math.log(0.8)

def matmul(left_side, right_side):
    return jnp.dot(left_side, right_side, precision=PRECISE, preferred_element_type=jnp.float32)

def orthogonal(basis_in):
    scaling = 0.4 / (jnp.sqrt(jnp.float32(basis_in.shape[0])) * jnp.sqrt(jnp.mean(basis_in * basis_in) + 1e-06))
    current = basis_in * scaling
    for _ in range(ITERS):
        gram_matrix = matmul(current.T, current)
        current = 1.5 * current - 0.5 * matmul(current, gram_matrix)
    return current

def soap_block(gradient, left_stat, right_stat, left_base, right_base, first_moment, second_moment, scale_factor):
    first_new = BETA_ONE * first_moment + (1.0 - BETA_ONE) * gradient
    grad_rot = matmul(matmul(left_base.T, gradient), right_base)
    first_rot = matmul(matmul(left_base.T, first_new), right_base)
    second_new = BETA_TWO * second_moment + (1.0 - BETA_TWO) * grad_rot * grad_rot
    normed = first_rot / (jnp.sqrt(second_new) + 1e-08)
    direction = matmul(matmul(left_base, normed), right_base.T)
    block_update = (scale_factor * direction).astype(jnp.bfloat16)
    left_new = BETA_TWO * left_stat + (1.0 - BETA_TWO) * matmul(gradient, gradient.T)
    right_new = BETA_TWO * right_stat + (1.0 - BETA_TWO) * matmul(gradient.T, gradient)
    left_base_new = orthogonal(matmul(left_new, left_base))
    right_base_new = orthogonal(matmul(right_new, right_base))
    return (block_update, left_new, right_new, left_base_new, right_base_new, first_new, second_new)

def slot_numbers(owner_device, capacity):
    block_count = owner_device.shape[0]
    same_owner = owner_device[:, None] == owner_device[None, :]
    earlier = jnp.arange(block_count)[None, :] < jnp.arange(block_count)[:, None]
    owner_rank = lax.optimization_barrier(jnp.sum((same_owner & earlier).astype(jnp.int32), axis=1)).astype(jnp.int32)
    return (owner_device * capacity + owner_rank).astype(jnp.int32)

def reference(partial_grads, owner_device, layer_of, stat_left, stat_right, basis_left, basis_right, moment_first, moment_second):
    slot_of = slot_numbers(owner_device, CAPD)
    layer_depth = (LAYERS - 1 - layer_of).astype(jnp.float32)
    factors = jnp.exp(SHRINK * layer_depth)

    def one_block(block_index):
        slot_place = slot_of[block_index]
        gradient = lax.optimization_barrier(jnp.sum(partial_grads[:, block_index].astype(jnp.float32), axis=0))
        return soap_block(gradient, stat_left[slot_place], stat_right[slot_place], basis_left[slot_place], basis_right[slot_place], moment_first[slot_place], moment_second[slot_place], factors[block_index])
    results = lax.map(one_block, jnp.arange(BLOCKS))
    olds = (stat_left, stat_right, basis_left, basis_right, moment_first, moment_second)
    news = tuple((old_state.at[slot_of].set(new_state) for old_state, new_state in zip(olds, results[1:])))
    return (results[0], news[0], news[1], news[2], news[3], news[4], news[5])
```

```python
import functools
import math

import jax
import jax.numpy as jnp
from jax import lax
from jax.experimental import pallas as pl
from jax.experimental.pallas import tpu as pltpu
from jax.sharding import PartitionSpec as P

ITERS = 4
BETA_ONE = 0.9
BETA_TWO = 0.95
SHRINK = math.log(0.8)
LANES = 128
TAIL = 16
MIB = 1 << 20
F32 = jnp.float32
BF16 = jnp.bfloat16
ANY = pl.BlockSpec(memory_space=pl.ANY)
SMEM = pl.BlockSpec(memory_space=pltpu.SMEM)


def params(limit=48 * MIB):
    return pltpu.CompilerParams(vmem_limit_bytes=limit)


def cost(flops, moved):
    return pl.CostEstimate(flops=int(flops), bytes_accessed=int(moved), transcendentals=0)


def table_kernel(devices, capacity, owner_ref, layer_ref, block_ref, rank_ref, count_ref, depth_ref):
    def clear(d, carry):
        count_ref[d] = 0
        for k in range(capacity):
            block_ref[k * devices + d] = 0
            depth_ref[k * devices + d] = 0
        return carry

    lax.fori_loop(0, devices, clear, 0)

    def place(b, carry):
        owner = owner_ref[b]
        rank = count_ref[owner]
        rank_ref[b] = rank
        block_ref[rank * devices + owner] = b
        depth_ref[rank * devices + owner] = layer_ref[b]
        count_ref[owner] = rank + 1
        return carry

    lax.fori_loop(0, owner_ref.shape[0], place, 0)


def tables(owner_device, layer_of, devices, capacity):
    blocks = owner_device.shape[0]
    flat = jax.ShapeDtypeStruct((capacity * devices,), jnp.int32)
    return pl.pallas_call(
        functools.partial(table_kernel, devices, capacity),
        out_shape=(
            flat,
            jax.ShapeDtypeStruct((blocks,), jnp.int32),
            jax.ShapeDtypeStruct((devices,), jnp.int32),
            flat,
        ),
        in_specs=[SMEM, SMEM],
        out_specs=(SMEM,) * 4,
        name="tables",
    )(owner_device, layer_of)


def pack_kernel(base, halves, members, place_ref, block_ref, grads_ref, out_ref, sems):
    def piece(i):
        group = place_ref[0] ^ (2 * (i // members) + 1)
        block = block_ref[base + group * members + i % members]
        return pltpu.make_async_copy(
            grads_ref.at[block], out_ref.at[i // members, i % members], sems.at[i]
        )

    def start(i, carry):
        piece(i).start()
        return carry

    def wait(i, carry):
        piece(i).wait()
        return carry

    lax.fori_loop(0, halves * members, start, 0)
    lax.fori_loop(0, halves * members, wait, 0)


def pack(rank, place, block_at, grads, halves, members, devices):
    rows, width = grads.shape[1:]
    return pl.pallas_call(
        functools.partial(pack_kernel, rank * devices, halves, members),
        out_shape=jax.ShapeDtypeStruct((halves, members, rows, width), grads.dtype),
        in_specs=[SMEM, SMEM, ANY],
        out_specs=ANY,
        scratch_shapes=[pltpu.SemaphoreType.DMA((halves * members,))],
        cost_estimate=cost(0, 4 * halves * members * rows * width),
        name="pack",
    )(place, block_at, grads)


def decode_scale(ref, lead, rows, panels):
    tail = ref[lead + (pl.ds(panels * rows, TAIL), slice(None))].astype(jnp.int32).astype(F32)
    power = jnp.concatenate([tail] * (LANES // TAIL), axis=0).T
    return jnp.exp2(-power[:rows])


def decode(ref, lead, rows, panel, scale):
    part = ref[lead + (pl.ds(panel * rows, rows), slice(None))]
    return part.astype(jnp.int32).astype(F32) * scale


def fold_kernel(earlier, tables_refs, raw_ref, core_ref, *refs):
    out_ref = refs[earlier]
    rows, width = raw_ref.shape[1:]
    panels = width // LANES
    total = raw_ref[0].astype(F32) + core_ref[0, 0].astype(F32)
    if earlier:
        parts = []
        scales = [decode_scale(refs[n], (0, 0), rows, panels) for n in range(earlier)]
        for p in range(panels):
            part = total[:, p * LANES : (p + 1) * LANES]
            for n in range(earlier):
                part = part + decode(refs[n], (0, 0), rows, p, scales[n])
            parts.append(part)
        total = jnp.concatenate(parts, axis=1)
    largest = jnp.max(jnp.abs(total), axis=1, keepdims=True)
    power = jnp.floor(14.99 - jnp.log2(jnp.maximum(largest, 1e-26)))
    scaled = jnp.round(total * jnp.exp2(power)).astype(jnp.int32)
    for p in range(panels):
        out_ref[0, 0, pl.ds(p * rows, rows), :] = scaled[:, p * LANES : (p + 1) * LANES].astype(jnp.int16)
    wide = jnp.broadcast_to(power, (rows, LANES))
    if rows < LANES:
        wide = jnp.concatenate([wide, jnp.zeros((LANES - rows, LANES), F32)], axis=0)
    out_ref[0, 0, pl.ds(panels * rows, TAIL), :] = wide.T[:TAIL].astype(jnp.int32).astype(jnp.int16)


def fold(rank, first, count, place, block_at, grads, from_core, from_x, members, devices):
    rows, width = grads.shape[1:]
    tall = (width // LANES) * rows + TAIL

    def raw_map(i, place_ref, block_ref):
        group = place_ref[0] ^ (2 * (first + i // members))
        return (block_ref[rank * devices + group * members + i % members], 0, 0)

    def sent_map(i, place_ref, block_ref):
        return (first + i // members, i % members, 0, 0)

    def out_map(i, place_ref, block_ref):
        return (i // members, i % members, 0, 0)

    def body(place_ref, block_ref, *refs):
        fold_kernel(len(from_x), None, *refs)

    return pl.pallas_call(
        body,
        grid_spec=pltpu.PrefetchScalarGridSpec(
            num_scalar_prefetch=2,
            grid=(count * members,),
            in_specs=[pl.BlockSpec((1, rows, width), raw_map), pl.BlockSpec((1, 1, rows, width), sent_map)]
            + [pl.BlockSpec((1, 1, tall, LANES), sent_map) for _ in from_x],
            out_specs=pl.BlockSpec((1, 1, tall, LANES), out_map),
        ),
        out_shape=jax.ShapeDtypeStruct((count, members, tall, LANES), jnp.int16),
        cost_estimate=cost(0, 8 * count * members * rows * width),
        name="fold",
    )(place, block_at, grads, from_core, *from_x)


def split(x):
    high = x.astype(BF16)
    return high, (x - high.astype(F32)).astype(BF16)


def put_cols(ref, rows, x, order):
    width = x.shape[1]
    pieces = split(x)
    for n, which in enumerate(order):
        ref[rows, pl.ds(n * width, width)] = pieces[which]


def put_rows(ref, start, height, x):
    high, low = split(x)
    size = x.shape[0]
    ref[pl.ds(start, size), :] = high
    ref[pl.ds(height + start, size), :] = low
    ref[pl.ds(2 * height + start, size), :] = high


def dot_nn(a, b):
    return lax.dot_general(a, b, (((1,), (0,)), ((), ())), preferred_element_type=F32)


def dot_nt(a, b):
    return lax.dot_general(a, b, (((1,), (1,)), ((), ())), preferred_element_type=F32)


LEFT = (0, 0, 1)
BOTH = (0, 0, 1, 0)


def tiles(height, size=256):
    return [pl.ds(s, size) for s in range(0, height, size)]


def update_kernel(rank, slot, info_ref, pay_ref, ql_ref, qr_ref, m_ref, v_ref, *refs):
    g_ref, u_ref, m1_ref, v1_ref, qlt_ref, ql3_ref, qrs_ref, qrp_ref, bs_ref, as_ref, mrot_ref = refs[-11:]
    width = g_ref.shape[0]
    members = pay_ref.shape[0]
    rows = width // members
    panels = width // LANES
    live = info_ref[0] > rank

    @pl.when(jnp.logical_not(live))
    def _():
        u_ref[...] = jnp.zeros_like(u_ref)
        m1_ref[0] = m_ref[0]
        v1_ref[0] = v_ref[0]

    @pl.when(live)
    def _():
        put_cols(qlt_ref, slice(None), ql_ref[0].T, LEFT)
        put_rows(qrs_ref, 0, width, qr_ref[0])

        def bring(member, carry):
            scale = decode_scale(pay_ref, (member,), rows, panels)
            at = pl.multiple_of(member * rows, rows)
            for p in range(panels):
                g_ref[pl.ds(at, rows), pl.ds(p * LANES, LANES)] = decode(pay_ref, (member,), rows, p, scale)
            return carry

        lax.fori_loop(0, members, bring, 0)
        m1_ref[0] = BETA_ONE * m_ref[0] + (1.0 - BETA_ONE) * g_ref[...]

        put_rows(bs_ref, 0, width, m1_ref[0])
        for t in tiles(width):
            put_cols(as_ref, t, dot_nn(qlt_ref[t, :], bs_ref[...]), LEFT)
        for t in tiles(width):
            mrot_ref[t, :] = dot_nn(as_ref[t, :], qrs_ref[...])

        put_rows(bs_ref, 0, width, g_ref[...])
        for t in tiles(width):
            put_cols(as_ref, t, dot_nn(qlt_ref[t, :], bs_ref[...]), LEFT)
        for t in tiles(width):
            rot = dot_nn(as_ref[t, :], qrs_ref[...])
            second = BETA_TWO * v_ref[0, t, :] + (1.0 - BETA_TWO) * rot * rot
            v1_ref[0, t, :] = second
            put_rows(bs_ref, t.start, width, mrot_ref[t, :] / (jnp.sqrt(second) + 1e-08))
        put_cols(ql3_ref, slice(None), ql_ref[0], LEFT)
        put_cols(qrp_ref, slice(None), qr_ref[0], (0, 1, 0))
        depth = info_ref[1].astype(F32)
        factor = jnp.exp(SHRINK * jnp.full((1, width), depth, F32))
        for t in tiles(width):
            put_cols(as_ref, t, dot_nn(ql3_ref[t, :], bs_ref[...]), LEFT)
        for t in tiles(width):
            u_ref[t, :] = (factor * dot_nt(as_ref[t, :], qrp_ref[...])).astype(BF16)


def slot_block(slot, width):
    return pl.BlockSpec((1, width, width), lambda *_: (slot, 0, 0))


def update_call(rank, info, pay, ql, qr, m, v, carried):
    width = ql.shape[1]
    own = slot_block(rank, width)
    whole = pl.BlockSpec((width, width), lambda *_: (0, 0))
    state = jax.ShapeDtypeStruct(m.shape, F32)
    operands = [info, pay, ql, qr, m, v] + list(carried)
    aliases = {6: 2, 7: 3} if carried else {}
    wide = lambda n: pltpu.VMEM((width, n * width), BF16)
    tall = pltpu.VMEM((3 * width, width), BF16)
    return pl.pallas_call(
        functools.partial(update_kernel, rank, rank),
        grid=(1,),
        out_shape=(
            jax.ShapeDtypeStruct((width, width), F32),
            jax.ShapeDtypeStruct((width, width), BF16),
            state,
            state,
        ),
        in_specs=[SMEM, pl.BlockSpec(pay.shape, lambda *_: (0, 0, 0)), own, own, own, own] + [ANY] * len(carried),
        out_specs=(whole, whole, own, own),
        scratch_shapes=[wide(3), wide(3), tall, wide(3), tall, wide(3), pltpu.VMEM((width, width), F32)],
        input_output_aliases=aliases,
        compiler_params=params(),
        cost_estimate=cost(6 * 3 * 2 * width**3, 10 * 4 * width**2),
        name="update",
    )(*operands)


def basis_kernel(rank, left, info_ref, g_ref, s_ref, q_ref, *refs):
    s1_ref, q1_ref, y_ref, cols_ref, a_ref, b_ref = refs[-6:]
    width = g_ref.shape[0]
    live = info_ref[0] > rank
    fits = pl.ds(0, 3 * width), pl.ds(width, 3 * width)

    @pl.when(jnp.logical_not(live))
    def _():
        s1_ref[0] = s_ref[0]
        q1_ref[0] = q_ref[0]

    @pl.when(live)
    def _():
        grad = g_ref[...] if left else g_ref[...].T
        put_cols(cols_ref, slice(None), grad, BOTH)
        put_cols(a_ref, slice(None), q_ref[0].T, LEFT)
        for t in tiles(width):
            outer = dot_nt(cols_ref[t, fits[0]], cols_ref[:, fits[1]])
            stat = BETA_TWO * s_ref[0, t, :] + (1.0 - BETA_TWO) * outer
            s1_ref[0, t, :] = stat
            put_rows(b_ref, t.start, width, stat)
        squares = jnp.zeros((1, width), F32)
        for t in tiles(width):
            turned = dot_nn(a_ref[t, :], b_ref[...])
            y_ref[t, :] = turned
            squares = squares + jnp.sum(turned * turned, axis=0, keepdims=True)
        mean = jnp.sum(squares, axis=1, keepdims=True) * (1.0 / (width * width))
        scaling = 0.4 / (math.sqrt(width) * jnp.sqrt(mean + 1e-06))
        y_ref[...] = y_ref[...] * scaling

        def step(i, carry):
            for t in tiles(width):
                put_cols(cols_ref, t, y_ref[t, :], BOTH)
                put_rows(b_ref, t.start, width, y_ref[t, :])
            for t in tiles(width):
                put_cols(a_ref, t, dot_nt(cols_ref[t, fits[0]], cols_ref[:, fits[1]]), LEFT)
            for t in tiles(width):
                y_ref[t, :] = 1.5 * y_ref[t, :] - 0.5 * dot_nn(a_ref[t, :], b_ref[...])
            return carry

        lax.fori_loop(0, ITERS, step, 0)
        q1_ref[0] = y_ref[...].T


def basis_call(rank, left, info, grad, stat, basis, carried):
    width = grad.shape[0]
    own = slot_block(rank, width)
    whole = pl.BlockSpec((width, width), lambda *_: (0, 0))
    state = jax.ShapeDtypeStruct(stat.shape, F32)
    return pl.pallas_call(
        functools.partial(basis_kernel, rank, left),
        grid=(1,),
        out_shape=(state, state),
        in_specs=[SMEM, whole, own, own] + [ANY] * len(carried),
        out_specs=(own, own),
        scratch_shapes=[
            pltpu.VMEM((width, width), F32),
            pltpu.VMEM((width, 4 * width), BF16),
            pltpu.VMEM((width, 3 * width), BF16),
            pltpu.VMEM((3 * width, width), BF16),
        ],
        input_output_aliases={4: 0, 5: 1} if carried else {},
        compiler_params=params(),
        cost_estimate=cost((2 + 2 * ITERS) * 3 * 2 * width**3, 5 * 4 * width**2),
        name="basis_left" if left else "basis_right",
    )(info, grad, stat, basis, *carried)


def pick_kernel(groups, members, count, place_ref, owner_ref, rank_ref, *refs):
    sources, out_ref, sems = refs[:-2], refs[-2], refs[-1]

    def start(i, carry):
        block = place_ref[0] * count + i
        owner = owner_ref[block]
        which = rank_ref[block] * groups + ((owner // members) ^ place_ref[0])
        for n, source in enumerate(sources):

            @pl.when(which == n)
            def _():
                pltpu.make_async_copy(source.at[owner % members], out_ref.at[i], sems.at[i]).start()

        return carry

    def wait(i, carry):
        pltpu.make_async_copy(sources[0].at[0], out_ref.at[i], sems.at[i]).wait()
        return carry

    lax.fori_loop(0, count, start, 0)
    lax.fori_loop(0, count, wait, 0)


def pick(place, owner_device, rank_of, sources, groups, members):
    rows, width = sources[0].shape[1:]
    count = owner_device.shape[0] // groups
    return pl.pallas_call(
        functools.partial(pick_kernel, groups, members, count),
        out_shape=jax.ShapeDtypeStruct((count, rows, width), BF16),
        in_specs=[SMEM] * 3 + [ANY] * len(sources),
        out_specs=ANY,
        scratch_shapes=[pltpu.SemaphoreType.DMA((count,))],
        cost_estimate=cost(0, 4 * count * rows * width),
        name="pick",
    )(place, owner_device, rank_of, *sources)


def local(
    partial_grads,
    owner_device,
    layer_of,
    stat_left,
    stat_right,
    basis_left,
    basis_right,
    moment_first,
    moment_second,
):
    capacity = stat_left.shape[0]
    width = stat_left.shape[1]
    groups = lax.axis_size("dp")
    members = lax.axis_size("mp")
    devices = groups * members
    halves = groups // 2
    grads = partial_grads[0]
    rows = grads.shape[1]
    place = jnp.reshape(lax.axis_index("dp"), (1,))
    own = lax.axis_index(("dp", "mp"))

    def flip(x, bits):
        return lax.ppermute(x, "dp", [(i, i ^ bits) for i in range(groups)])

    block_at, rank_of, counts, layer_at = tables(owner_device, layer_of, devices, capacity)
    own_count = lax.dynamic_index_in_dim(counts, own, keepdims=False)

    infos, from_core = [], []
    for k in range(capacity):
        layer = lax.dynamic_index_in_dim(layer_at, k * devices + own, keepdims=False)
        infos.append(jnp.stack([own_count, groups - 1 - layer]))
        from_core.append(flip(pack(k, place, block_at, grads, halves, members, devices), 1))

    arrived = []
    for k in range(capacity):
        from_x = []
        step = halves // 2
        while step:
            sent = fold(k, step, step, place, block_at, grads, from_core[k], from_x, members, devices)
            from_x.append(flip(sent, 2 * step))
            step //= 2
        ready = fold(k, 0, 1, place, block_at, grads, from_core[k], from_x, members, devices)
        arrived.append(lax.all_to_all(ready[0], "mp", split_axis=0, concat_axis=0, tiled=True))

    sources, gradients, moments = [], [], ()
    for k in range(capacity):
        grad, block_update, *moments = update_call(
            k, infos[k], arrived[k], basis_left, basis_right, moment_first, moment_second, tuple(moments)
        )
        gradients.append(grad)
        pieces = lax.all_to_all(
            block_update.reshape(members, rows, width), "mp", split_axis=0, concat_axis=0, tiled=True
        )
        held = [pieces]
        step = 1
        while step < halves:
            held = held + [flip(part, 2 * step) for part in held]
            step *= 2
        for part in held:
            sources += [part, flip(part, 1)]

    lefts, rights = (), ()
    for k in range(capacity):
        lefts = basis_call(k, True, infos[k], gradients[k], stat_left, basis_left, tuple(lefts))
        rights = basis_call(k, False, infos[k], gradients[k], stat_right, basis_right, tuple(rights))

    update_rows = pick(place, owner_device, rank_of, sources, groups, members)
    return (update_rows, lefts[0], rights[0], lefts[1], rights[1], moments[0], moments[1])


def solution(mesh):
    slots = P(("dp", "mp"), None, None)
    in_specs = (P("dp", None, "mp", None), P(), P()) + (slots,) * 6
    out_specs = (P("dp", "mp", None),) + (slots,) * 6
    return jax.shard_map(local, mesh=mesh, in_specs=in_specs, out_specs=out_specs, check_vma=False)
```

```python
import functools
import math

import jax
import jax.numpy as jnp
from jax import lax
from jax.experimental import pallas as pl
from jax.experimental.pallas import tpu as pltpu
from jax.sharding import PartitionSpec as P

ITERS = 4
BETA_ONE = 0.9
BETA_TWO = 0.95
SHRINK = math.log(0.8)
LANES = 128
TAIL = 16
MIB = 1 << 20
F32 = jnp.float32
BF16 = jnp.bfloat16
ANY = pl.BlockSpec(memory_space=pl.ANY)
SMEM = pl.BlockSpec(memory_space=pltpu.SMEM)


def params(limit=60 * MIB):
    return pltpu.CompilerParams(vmem_limit_bytes=limit)


def cost(flops, moved):
    return pl.CostEstimate(flops=int(flops), bytes_accessed=int(moved), transcendentals=0)


def gather(base, halves, members, place_ref, block_ref, grads_ref, out_ref, sems):
    copies = []
    for i in range(halves * members):
        group = place_ref[0] ^ (2 * (i // members) + 1)
        block = block_ref[base + group * members + i % members]
        copies.append(
            pltpu.make_async_copy(grads_ref.at[block], out_ref.at[i // members, i % members], sems.at[i])
        )
        copies[-1].start()
    for copy in copies:
        copy.wait()


def route_kernel(
    capacity, halves, members, owner_ref, layer_ref, place_ref, grads_ref,
    block_ref, rank_ref, count_ref, depth_ref, out_ref, sems,
):
    devices = 2 * halves * members
    for d in range(devices):
        count_ref[d] = 0
        for k in range(capacity):
            block_ref[k * devices + d] = 0
            depth_ref[k * devices + d] = 0
    for b in range(owner_ref.shape[0]):
        owner = owner_ref[b]
        rank = count_ref[owner]
        rank_ref[b] = rank
        block_ref[rank * devices + owner] = b
        depth_ref[rank * devices + owner] = layer_ref[b]
        count_ref[owner] = rank + 1
    gather(0, halves, members, place_ref, block_ref, grads_ref, out_ref, sems)


def route(owner_device, layer_of, place, grads, capacity, halves, members):
    devices = 2 * halves * members
    packed = (halves, members) + grads.shape[1:]
    flat = jax.ShapeDtypeStruct((capacity * devices,), jnp.int32)
    return pl.pallas_call(
        functools.partial(route_kernel, capacity, halves, members),
        out_shape=(
            flat,
            jax.ShapeDtypeStruct(owner_device.shape, jnp.int32),
            jax.ShapeDtypeStruct((devices,), jnp.int32),
            flat,
            jax.ShapeDtypeStruct(packed, grads.dtype),
        ),
        in_specs=[SMEM, SMEM, SMEM, ANY],
        out_specs=(SMEM,) * 4 + (pl.BlockSpec(memory_space=pltpu.VMEM),),
        scratch_shapes=[pltpu.SemaphoreType.DMA((halves * members,))],
        compiler_params=params(),
        cost_estimate=cost(0, 4 * math.prod(packed)),
        name="route",
    )(owner_device, layer_of, place, grads)


def pack(rank, place, block_at, grads, halves, members):
    packed = (halves, members) + grads.shape[1:]
    return pl.pallas_call(
        functools.partial(gather, rank * 2 * halves * members, halves, members),
        out_shape=jax.ShapeDtypeStruct(packed, grads.dtype),
        in_specs=[SMEM, SMEM, ANY],
        out_specs=pl.BlockSpec(memory_space=pltpu.VMEM),
        scratch_shapes=[pltpu.SemaphoreType.DMA((halves * members,))],
        compiler_params=params(),
        cost_estimate=cost(0, 4 * math.prod(packed)),
        name="pack",
    )(place, block_at, grads)


def decode_scale(ref, lead, rows, panels):
    tail = ref[lead + (pl.ds(panels * rows, TAIL), slice(None))].astype(jnp.int32).astype(F32)
    power = jnp.concatenate([tail] * (LANES // TAIL), axis=0).T
    return jnp.exp2(-power[:rows])


def decode(ref, lead, rows, panel, scale):
    part = ref[lead + (pl.ds(panel * rows, rows), slice(None))]
    return part.astype(jnp.int32).astype(F32) * scale


def fold_kernel(base, first, members, place_ref, block_ref, grads_ref, core_ref, *refs):
    earlier, (out_ref, raw_ref, sems) = refs[:-3], refs[-3:]
    count = out_ref.shape[0]
    rows, width = raw_ref.shape[1:]
    panels = width // LANES
    copies = []
    for i in range(count * members):
        group = place_ref[0] ^ (2 * (first + i // members))
        block = block_ref[base + group * members + i % members]
        copies.append(pltpu.make_async_copy(grads_ref.at[block], raw_ref.at[i], sems.at[i]))
        copies[-1].start()
    for copy in copies:
        copy.wait()

    def piece(i, carry):
        at = (i // members, i % members)
        total = raw_ref[i].astype(F32) + core_ref[at].astype(F32)
        parts = [total[:, p * LANES : (p + 1) * LANES] for p in range(panels)]
        for ref in earlier:
            scale = decode_scale(ref, at, rows, panels)
            parts = [part + decode(ref, at, rows, p, scale) for p, part in enumerate(parts)]
        largest = functools.reduce(jnp.maximum, [jnp.abs(part) for part in parts])
        largest = jnp.max(largest, axis=1, keepdims=True)
        power = jnp.floor(14.99 - jnp.log2(jnp.maximum(largest, 1e-26)))
        wide = jnp.broadcast_to(power, (rows, LANES))
        scale = jnp.exp2(wide)
        for p, part in enumerate(parts):
            out_ref[at + (pl.ds(p * rows, rows), slice(None))] = (
                jnp.round(part * scale).astype(jnp.int32).astype(jnp.int16)
            )
        if rows < LANES:
            wide = jnp.concatenate([wide, jnp.zeros((LANES - rows, LANES), F32)], axis=0)
        out_ref[at + (pl.ds(panels * rows, TAIL), slice(None))] = (
            wide.T[:TAIL].astype(jnp.int32).astype(jnp.int16)
        )
        return carry

    lax.fori_loop(0, count * members, piece, 0)


def fold(rank, first, count, place, block_at, grads, from_core, from_x, members):
    rows, width = grads.shape[1:]
    tall = (width // LANES) * rows + TAIL
    devices = 2 * from_core.shape[0] * members
    at = first // count
    return pl.pallas_call(
        functools.partial(fold_kernel, rank * devices, first, members),
        grid=(1,),
        in_specs=[SMEM, SMEM, ANY, pl.BlockSpec((count, members, rows, width), lambda i: (at, 0, 0, 0))]
        + [pl.BlockSpec((count, members, tall, LANES), lambda i: (at, 0, 0, 0)) for _ in from_x],
        out_specs=pl.BlockSpec((count, members, tall, LANES), lambda i: (0, 0, 0, 0)),
        out_shape=jax.ShapeDtypeStruct((count, members, tall, LANES), jnp.int16),
        scratch_shapes=[
            pltpu.VMEM((count * members, rows, width), grads.dtype),
            pltpu.SemaphoreType.DMA((count * members,)),
        ],
        compiler_params=params(),
        cost_estimate=cost(0, 8 * count * members * rows * width),
        name="fold",
    )(place, block_at, grads, from_core, *from_x)


def split(x):
    high = x.astype(BF16)
    return high, (x - high.astype(F32)).astype(BF16)


def put_cols(ref, rows, x, order):
    width = x.shape[1]
    pieces = split(x)
    for n, which in enumerate(order):
        ref[rows, pl.ds(n * width, width)] = pieces[which]


def put_rows(ref, start, height, x):
    high, low = split(x)
    size = x.shape[0]
    ref[pl.ds(start, size), :] = high
    ref[pl.ds(height + start, size), :] = low
    ref[pl.ds(2 * height + start, size), :] = high


def dot_nn(a, b):
    return lax.dot_general(a, b, (((1,), (0,)), ((), ())), preferred_element_type=F32)


def dot_nt(a, b):
    return lax.dot_general(a, b, (((1,), (1,)), ((), ())), preferred_element_type=F32)


LEFT = (0, 0, 1)
BOTH = (0, 0, 1, 0)


def tiles(height, size=256):
    return [pl.ds(s, size) for s in range(0, height, size)]


def update_kernel(rank, base, place_ref, count_ref, depth_ref, pay_ref, ql_ref, qr_ref, m_ref, v_ref, *refs):
    g_ref, u_ref, m1_ref, v1_ref, qlt_ref, ql3_ref, qrs_ref, qrp_ref, bs_ref, as_ref, mrot_ref = refs[-11:]
    width = g_ref.shape[0]
    members = pay_ref.shape[0]
    rows = width // members
    panels = width // LANES
    live = count_ref[place_ref[1]] > rank

    @pl.when(jnp.logical_not(live))
    def _():
        u_ref[...] = jnp.zeros_like(u_ref)
        m1_ref[0] = m_ref[0]
        v1_ref[0] = v_ref[0]

    @pl.when(live)
    def _():
        put_cols(qlt_ref, slice(None), ql_ref[0].T, LEFT)
        put_rows(qrs_ref, 0, width, qr_ref[0])

        def bring(member, carry):
            scale = decode_scale(pay_ref, (member,), rows, panels)
            at = pl.multiple_of(member * rows, rows)
            for p in range(panels):
                g_ref[pl.ds(at, rows), pl.ds(p * LANES, LANES)] = decode(pay_ref, (member,), rows, p, scale)
            return carry

        lax.fori_loop(0, members, bring, 0)
        m1_ref[0] = BETA_ONE * m_ref[0] + (1.0 - BETA_ONE) * g_ref[...]

        put_rows(bs_ref, 0, width, m1_ref[0])
        for t in tiles(width):
            put_cols(as_ref, t, dot_nn(qlt_ref[t, :], bs_ref[...]), LEFT)
        for t in tiles(width):
            mrot_ref[t, :] = dot_nn(as_ref[t, :], qrs_ref[...])

        put_rows(bs_ref, 0, width, g_ref[...])
        for t in tiles(width):
            put_cols(as_ref, t, dot_nn(qlt_ref[t, :], bs_ref[...]), LEFT)
        for t in tiles(width):
            rot = dot_nn(as_ref[t, :], qrs_ref[...])
            second = BETA_TWO * v_ref[0, t, :] + (1.0 - BETA_TWO) * rot * rot
            v1_ref[0, t, :] = second
            put_rows(bs_ref, t.start, width, mrot_ref[t, :] / (jnp.sqrt(second) + 1e-08))
        put_cols(ql3_ref, slice(None), ql_ref[0], LEFT)
        put_cols(qrp_ref, slice(None), qr_ref[0], (0, 1, 0))
        depth = (place_ref[2] - 1 - depth_ref[base + place_ref[1]]).astype(F32)
        factor = jnp.exp(SHRINK * jnp.full((1, width), depth, F32))
        for t in tiles(width):
            put_cols(as_ref, t, dot_nn(ql3_ref[t, :], bs_ref[...]), LEFT)
        for t in tiles(width):
            u_ref[t, :] = (factor * dot_nt(as_ref[t, :], qrp_ref[...])).astype(BF16)


def slot_block(slot, width):
    return pl.BlockSpec((1, width, width), lambda *_: (slot, 0, 0))


def update_call(rank, info, pay, ql, qr, m, v, carried):
    width = ql.shape[1]
    own = slot_block(rank, width)
    whole = pl.BlockSpec((width, width), lambda *_: (0, 0))
    state = jax.ShapeDtypeStruct(m.shape, F32)
    operands = list(info) + [pay, ql, qr, m, v] + list(carried)
    aliases = {8: 2, 9: 3} if carried else {}
    wide = lambda n: pltpu.VMEM((width, n * width), BF16)
    tall = pltpu.VMEM((3 * width, width), BF16)
    return pl.pallas_call(
        functools.partial(update_kernel, rank, rank * info[1].shape[0]),
        grid=(1,),
        out_shape=(
            jax.ShapeDtypeStruct((width, width), F32),
            jax.ShapeDtypeStruct((width, width), BF16),
            state,
            state,
        ),
        in_specs=[SMEM] * 3 + [pl.BlockSpec(pay.shape, lambda *_: (0, 0, 0)), own, own, own, own] + [ANY] * len(carried),
        out_specs=(whole, whole, own, own),
        scratch_shapes=[wide(3), wide(3), tall, wide(3), tall, wide(3), pltpu.VMEM((width, width), F32)],
        input_output_aliases=aliases,
        compiler_params=params(),
        cost_estimate=cost(6 * 3 * 2 * width**3, 10 * 4 * width**2),
        name="update",
    )(*operands)


def basis_kernel(rank, left, place_ref, count_ref, g_ref, s_ref, q_ref, *refs):
    s1_ref, q1_ref, y_ref, cols_ref, a_ref, b_ref = refs[-6:]
    width = g_ref.shape[0]
    live = count_ref[place_ref[1]] > rank
    fits = pl.ds(0, 3 * width), pl.ds(width, 3 * width)

    @pl.when(jnp.logical_not(live))
    def _():
        s1_ref[0] = s_ref[0]
        q1_ref[0] = q_ref[0]

    @pl.when(live)
    def _():
        grad = g_ref[...] if left else g_ref[...].T
        put_cols(cols_ref, slice(None), grad, BOTH)
        put_cols(a_ref, slice(None), q_ref[0].T, LEFT)
        for t in tiles(width):
            outer = dot_nt(cols_ref[t, fits[0]], cols_ref[:, fits[1]])
            stat = BETA_TWO * s_ref[0, t, :] + (1.0 - BETA_TWO) * outer
            s1_ref[0, t, :] = stat
            put_rows(b_ref, t.start, width, stat)
        squares = jnp.zeros((1, width), F32)
        for t in tiles(width):
            turned = dot_nn(a_ref[t, :], b_ref[...])
            y_ref[t, :] = turned
            squares = squares + jnp.sum(turned * turned, axis=0, keepdims=True)
        mean = jnp.sum(squares, axis=1, keepdims=True) * (1.0 / (width * width))
        scaling = 0.4 / (math.sqrt(width) * jnp.sqrt(mean + 1e-06))
        y_ref[...] = y_ref[...] * scaling

        def step(i, carry):
            for t in tiles(width):
                put_cols(cols_ref, t, y_ref[t, :], BOTH)
                put_rows(b_ref, t.start, width, y_ref[t, :])
            for t in tiles(width):
                put_cols(a_ref, t, dot_nt(cols_ref[t, fits[0]], cols_ref[:, fits[1]]), LEFT)
            for t in tiles(width):
                y_ref[t, :] = 1.5 * y_ref[t, :] - 0.5 * dot_nn(a_ref[t, :], b_ref[...])
            return carry

        lax.fori_loop(0, ITERS, step, 0)
        q1_ref[0] = y_ref[...].T


def basis_call(rank, left, info, grad, stat, basis, carried):
    width = grad.shape[0]
    own = slot_block(rank, width)
    whole = pl.BlockSpec((width, width), lambda *_: (0, 0))
    state = jax.ShapeDtypeStruct(stat.shape, F32)
    return pl.pallas_call(
        functools.partial(basis_kernel, rank, left),
        grid=(1,),
        out_shape=(state, state),
        in_specs=[SMEM, SMEM, whole, own, own] + [ANY] * len(carried),
        out_specs=(own, own),
        scratch_shapes=[
            pltpu.VMEM((width, width), F32),
            pltpu.VMEM((width, 4 * width), BF16),
            pltpu.VMEM((width, 3 * width), BF16),
            pltpu.VMEM((3 * width, width), BF16),
        ],
        input_output_aliases={5: 0, 6: 1} if carried else {},
        compiler_params=params(),
        cost_estimate=cost((2 + 2 * ITERS) * 3 * 2 * width**3, 5 * 4 * width**2),
        name="basis_left" if left else "basis_right",
    )(*info[:2], grad, stat, basis, *carried)


def pick_kernel(groups, members, count, place_ref, owner_ref, rank_ref, *refs):
    sources, out_ref, sems = refs[:-2], refs[-2], refs[-1]

    def start(i, carry):
        block = place_ref[0] * count + i
        owner = owner_ref[block]
        which = rank_ref[block] * groups + ((owner // members) ^ place_ref[0])
        for n, source in enumerate(sources):

            @pl.when(which == n)
            def _():
                pltpu.make_async_copy(source.at[owner % members], out_ref.at[i], sems.at[i]).start()

        return carry

    def wait(i, carry):
        pltpu.make_async_copy(sources[0].at[0], out_ref.at[i], sems.at[i]).wait()
        return carry

    lax.fori_loop(0, count, start, 0)
    lax.fori_loop(0, count, wait, 0)


def pick(place, owner_device, rank_of, sources, groups, members):
    rows, width = sources[0].shape[1:]
    count = owner_device.shape[0] // groups
    return pl.pallas_call(
        functools.partial(pick_kernel, groups, members, count),
        out_shape=jax.ShapeDtypeStruct((count, rows, width), BF16),
        in_specs=[SMEM] * 3 + [ANY] * len(sources),
        out_specs=pl.BlockSpec(memory_space=pltpu.VMEM),
        scratch_shapes=[pltpu.SemaphoreType.DMA((count,))],
        compiler_params=params(),
        cost_estimate=cost(0, 4 * count * rows * width),
        name="pick",
    )(place, owner_device, rank_of, *sources)


def local(
    partial_grads,
    owner_device,
    layer_of,
    stat_left,
    stat_right,
    basis_left,
    basis_right,
    moment_first,
    moment_second,
):
    capacity = stat_left.shape[0]
    width = stat_left.shape[1]
    groups = lax.axis_size("dp")
    members = lax.axis_size("mp")
    halves = groups // 2
    grads = partial_grads[0]
    rows = grads.shape[1]
    own = lax.axis_index(("dp", "mp"))
    place = jnp.stack([lax.axis_index("dp"), own, groups])

    def flip(x, bits):
        return lax.ppermute(x, "dp", [(i, i ^ bits) for i in range(groups)])

    block_at, rank_of, counts, layer_at, packed = route(
        owner_device, layer_of, place, grads, capacity, halves, members
    )
    info = (place, counts, layer_at)
    from_core = [flip(packed, 1)]
    for k in range(1, capacity):
        from_core.append(flip(pack(k, place, block_at, grads, halves, members), 1))

    arrived = []
    for k in range(capacity):
        from_x = []
        step = halves // 2
        while step:
            sent = fold(k, step, step, place, block_at, grads, from_core[k], from_x, members)
            from_x.append(flip(sent, 2 * step))
            step //= 2
        ready = fold(k, 0, 1, place, block_at, grads, from_core[k], from_x, members)
        arrived.append(lax.all_to_all(ready[0], "mp", split_axis=0, concat_axis=0, tiled=True))

    sources, gradients, moments = [], [], ()
    for k in range(capacity):
        grad, block_update, *moments = update_call(
            k, info, arrived[k], basis_left, basis_right, moment_first, moment_second, tuple(moments)
        )
        gradients.append(grad)
        pieces = lax.all_to_all(
            block_update.reshape(members, rows, width), "mp", split_axis=0, concat_axis=0, tiled=True
        )
        held = [pieces]
        step = 1
        while step < halves:
            held = held + [flip(part, 2 * step) for part in held]
            step *= 2
        for part in held:
            sources += [part, flip(part, 1)]

    lefts, rights = (), ()
    for k in range(capacity):
        lefts = basis_call(k, True, info, gradients[k], stat_left, basis_left, tuple(lefts))
        rights = basis_call(k, False, info, gradients[k], stat_right, basis_right, tuple(rights))

    update_rows = pick(place, owner_device, rank_of, sources, groups, members)
    return (update_rows, lefts[0], rights[0], lefts[1], rights[1], moments[0], moments[1])


def solution(mesh):
    slots = P(("dp", "mp"), None, None)
    in_specs = (P("dp", None, "mp", None), P(), P()) + (slots,) * 6
    out_specs = (P("dp", "mp", None),) + (slots,) * 6
    return jax.shard_map(local, mesh=mesh, in_specs=in_specs, out_specs=out_specs, check_vma=False)
```

```python
import functools
import math

import jax
import jax.numpy as jnp
from jax import lax
from jax.experimental import pallas as pl
from jax.experimental.pallas import tpu as pltpu
from jax.sharding import PartitionSpec as P

ITERS = 4
BETA_ONE = 0.9
BETA_TWO = 0.95
SHRINK = math.log(0.8)
LANES = 128
TAIL = 16
MIB = 1 << 20
ROOMY = 24 * MIB
WEIGHT = 1.0
F32 = jnp.float32
BF16 = jnp.bfloat16
ANY = pl.BlockSpec(memory_space=pl.ANY)
SMEM = pl.BlockSpec(memory_space=pltpu.SMEM)


def params(limit=60 * MIB):
    return pltpu.CompilerParams(vmem_limit_bytes=limit)


def cost(flops, moved):
    return pl.CostEstimate(flops=int(flops * WEIGHT), bytes_accessed=int(moved * WEIGHT), transcendentals=0)


def gather(base, halves, members, place_ref, block_ref, grads_ref, out_ref, sems):
    copies = []
    for i in range(halves * members):
        group = place_ref[0] ^ (2 * (i // members) + 1)
        block = block_ref[base + group * members + i % members]
        copies.append(
            pltpu.make_async_copy(grads_ref.at[block], out_ref.at[i // members, i % members], sems.at[i])
        )
        copies[-1].start()
    for copy in copies:
        copy.wait()


def route_kernel(
    capacity, halves, members, owner_ref, layer_ref, place_ref, grads_ref,
    block_ref, rank_ref, count_ref, depth_ref, out_ref, sems,
):
    devices = 2 * halves * members
    for d in range(devices):
        count_ref[d] = 0
        for k in range(capacity):
            block_ref[k * devices + d] = 0
            depth_ref[k * devices + d] = 0
    for b in range(owner_ref.shape[0]):
        owner = owner_ref[b]
        rank = count_ref[owner]
        rank_ref[b] = rank
        block_ref[rank * devices + owner] = b
        depth_ref[rank * devices + owner] = layer_ref[b]
        count_ref[owner] = rank + 1
    gather(0, halves, members, place_ref, block_ref, grads_ref, out_ref, sems)


def route(owner_device, layer_of, place, grads, capacity, halves, members):
    devices = 2 * halves * members
    packed = (halves, members) + grads.shape[1:]
    flat = jax.ShapeDtypeStruct((capacity * devices,), jnp.int32)
    return pl.pallas_call(
        functools.partial(route_kernel, capacity, halves, members),
        out_shape=(
            flat,
            jax.ShapeDtypeStruct(owner_device.shape, jnp.int32),
            jax.ShapeDtypeStruct((devices,), jnp.int32),
            flat,
            jax.ShapeDtypeStruct(packed, grads.dtype),
        ),
        in_specs=[SMEM, SMEM, SMEM, ANY],
        out_specs=(SMEM,) * 4 + (pl.BlockSpec(memory_space=pltpu.VMEM),),
        scratch_shapes=[pltpu.SemaphoreType.DMA((halves * members,))],
        compiler_params=params(),
        cost_estimate=cost(0, 4 * math.prod(packed)),
        name="route",
    )(owner_device, layer_of, place, grads)


def pack(rank, place, block_at, grads, halves, members):
    packed = (halves, members) + grads.shape[1:]
    return pl.pallas_call(
        functools.partial(gather, rank * 2 * halves * members, halves, members),
        out_shape=jax.ShapeDtypeStruct(packed, grads.dtype),
        in_specs=[SMEM, SMEM, ANY],
        out_specs=pl.BlockSpec(memory_space=pltpu.VMEM),
        scratch_shapes=[pltpu.SemaphoreType.DMA((halves * members,))],
        compiler_params=params(),
        cost_estimate=cost(0, 4 * math.prod(packed)),
        name="pack",
    )(place, block_at, grads)


def decode_scale(ref, lead, rows, panels):
    tail = ref[lead + (pl.ds(panels * rows, TAIL), slice(None))].astype(jnp.int32).astype(F32)
    power = jnp.concatenate([tail] * (LANES // TAIL), axis=0).T
    return jnp.exp2(-power[:rows])


def decode(ref, lead, rows, panel, scale):
    part = ref[lead + (pl.ds(panel * rows, rows), slice(None))]
    return part.astype(jnp.int32).astype(F32) * scale


def fold_kernel(base, first, members, earlier_count, place_ref, block_ref, grads_ref, core_ref, *refs):
    earlier, (out_ref, done_ref, raw_ref, sems) = refs[:earlier_count], refs[-4:]
    done_ref[0] = 1
    count = out_ref.shape[0]
    rows, width = raw_ref.shape[1:]
    panels = width // LANES
    for i in range(count * members):
        group = place_ref[0] ^ (2 * (first + i // members))
        block = block_ref[base + group * members + i % members]
        pltpu.make_async_copy(grads_ref.at[block], raw_ref.at[i], sems.at[i]).start()

    def piece(i, carry):
        pltpu.make_async_copy(grads_ref.at[0], raw_ref.at[i], sems.at[i]).wait()
        at = (i // members, i % members)
        total = raw_ref[i].astype(F32) + core_ref[at].astype(F32)
        parts = [total[:, p * LANES : (p + 1) * LANES] for p in range(panels)]
        for ref in earlier:
            scale = decode_scale(ref, at, rows, panels)
            parts = [part + decode(ref, at, rows, p, scale) for p, part in enumerate(parts)]
        largest = functools.reduce(jnp.maximum, [jnp.abs(part) for part in parts])
        largest = jnp.max(largest, axis=1, keepdims=True)
        power = jnp.floor(14.99 - jnp.log2(jnp.maximum(largest, 1e-26)))
        wide = jnp.broadcast_to(power, (rows, LANES))
        scale = jnp.exp2(wide)
        for p, part in enumerate(parts):
            out_ref[at + (pl.ds(p * rows, rows), slice(None))] = (
                jnp.round(part * scale).astype(jnp.int32).astype(jnp.int16)
            )
        if rows < LANES:
            wide = jnp.concatenate([wide, jnp.zeros((LANES - rows, LANES), F32)], axis=0)
        out_ref[at + (pl.ds(panels * rows, TAIL), slice(None))] = (
            wide.T[:TAIL].astype(jnp.int32).astype(jnp.int16)
        )
        return carry

    lax.fori_loop(0, count * members, piece, 0)


def fold(rank, first, count, place, block_at, grads, from_core, from_x, members, after=()):
    rows, width = grads.shape[1:]
    tall = (width // LANES) * rows + TAIL
    devices = 2 * from_core.shape[0] * members
    at = first // count
    return pl.pallas_call(
        functools.partial(fold_kernel, rank * devices, first, members, len(from_x)),
        grid=(1,),
        in_specs=[SMEM, SMEM, ANY, pl.BlockSpec((count, members, rows, width), lambda i: (at, 0, 0, 0))]
        + [pl.BlockSpec((count, members, tall, LANES), lambda i: (at, 0, 0, 0)) for _ in from_x]
        + [SMEM] * len(after),
        out_specs=(pl.BlockSpec((count, members, tall, LANES), lambda i: (0, 0, 0, 0)), SMEM),
        out_shape=(
            jax.ShapeDtypeStruct((count, members, tall, LANES), jnp.int16),
            jax.ShapeDtypeStruct((1,), jnp.int32),
        ),
        scratch_shapes=[
            pltpu.VMEM((count * members, rows, width), grads.dtype),
            pltpu.SemaphoreType.DMA((count * members,)),
        ],
        compiler_params=params(ROOMY),
        cost_estimate=cost(0, 8 * count * members * rows * width),
        name="fold",
    )(place, block_at, grads, from_core, *from_x, *after)


def split(x):
    high = x.astype(BF16)
    return high, (x - high.astype(F32)).astype(BF16)


def put_cols(ref, rows, x, order):
    width = x.shape[1]
    pieces = split(x)
    for n, which in enumerate(order):
        ref[rows, pl.ds(n * width, width)] = pieces[which]


def put_rows(ref, start, height, x):
    high, low = split(x)
    size = x.shape[0]
    ref[pl.ds(start, size), :] = high
    ref[pl.ds(height + start, size), :] = low
    ref[pl.ds(2 * height + start, size), :] = high


def dot_nn(a, b):
    return lax.dot_general(a, b, (((1,), (0,)), ((), ())), preferred_element_type=F32)


def dot_nt(a, b):
    return lax.dot_general(a, b, (((1,), (1,)), ((), ())), preferred_element_type=F32)


LEFT = (0, 0, 1)
BOTH = (0, 0, 1, 0)


def tiles(height, size=512):
    return [pl.ds(s, size) for s in range(0, height, size)]


class Copies:
    def __init__(self, sems):
        self.sems, self.used = sems, 0

    def start(self, source, target):
        copy = pltpu.make_async_copy(source, target, self.sems.at[self.used])
        self.used += 1
        copy.start()
        return copy


def premix_kernel(slots, place_ref, count_ref, ql_hbm, qr_hbm, m_hbm, *refs):
    mq_hbm, done_ref, ql_ref, qr_ref, m_ref, qlt_ref, b_ref, a_ref, sems = refs[-9:]
    width = ql_ref.shape[0]
    done_ref[0] = 1
    for slot in range(slots):

        @pl.when(count_ref[place_ref[1]] > slot)
        def _():
            copies = Copies(sems)
            load_m = copies.start(m_hbm.at[slot], m_ref)
            load_l = copies.start(ql_hbm.at[slot], ql_ref)
            load_r = copies.start(qr_hbm.at[slot], qr_ref)
            load_m.wait()
            put_rows(b_ref, 0, width, m_ref[...])
            load_l.wait()
            put_cols(qlt_ref, slice(None), ql_ref[...].T, LEFT)
            for t in tiles(width):
                put_cols(a_ref, t, dot_nn(qlt_ref[t, :], b_ref[...]), LEFT)
            load_r.wait()
            put_rows(b_ref, 0, width, qr_ref[...])
            for t in tiles(width):
                m_ref[t, :] = dot_nn(a_ref[t, :], b_ref[...])
            copies.start(m_ref, mq_hbm.at[slot]).wait()


def premix(place, counts, ql, qr, m, after):
    slots, width = ql.shape[:2]
    flat = pltpu.VMEM((width, width), F32)
    wide = pltpu.VMEM((width, 3 * width), BF16)
    tall = pltpu.VMEM((3 * width, width), BF16)
    return pl.pallas_call(
        functools.partial(premix_kernel, slots),
        out_shape=(jax.ShapeDtypeStruct(m.shape, F32), jax.ShapeDtypeStruct((1,), jnp.int32)),
        in_specs=[SMEM, SMEM] + [ANY] * 3 + [SMEM] * len(after),
        out_specs=(ANY, SMEM),
        scratch_shapes=[flat, flat, flat, wide, tall, wide, pltpu.SemaphoreType.DMA((4,))],
        compiler_params=params(),
        cost_estimate=cost(slots * 2 * 3 * 2 * width**3, slots * 4 * 4 * width**2),
        name="premix",
    )(place, counts, ql, qr, m, *after)


def update_kernel(rank, base, place_ref, count_ref, depth_ref, pay_ref, ql_hbm, qr_hbm, m_hbm, v_hbm, mq_hbm, *refs):
    g_hbm, u_hbm, m1_hbm, v1_hbm = refs[-20:-16]
    g_ref, u_ref, ql_ref, qr_ref, m_ref, v_ref, mq_ref, qlt_ref, ql3_ref, qrs_ref, qrp_ref, bs_ref, bn_ref, as_ref, ab_ref, sems = refs[-16:]
    width = g_ref.shape[0]
    members = pay_ref.shape[0]
    rows = width // members
    panels = width // LANES
    live = count_ref[place_ref[1]] > rank

    @pl.when(jnp.logical_not(live))
    def _():
        copies = Copies(sems)
        loads = [copies.start(m_hbm.at[rank], m_ref), copies.start(v_hbm.at[rank], v_ref)]
        u_ref[...] = jnp.zeros_like(u_ref)
        stores = [copies.start(u_ref, u_hbm)]
        for load in loads:
            load.wait()
        stores += [copies.start(m_ref, m1_hbm.at[rank]), copies.start(v_ref, v1_hbm.at[rank])]
        for store in stores:
            store.wait()

    @pl.when(live)
    def _():
        copies = Copies(sems)
        load_l = copies.start(ql_hbm.at[rank], ql_ref)
        load_r = copies.start(qr_hbm.at[rank], qr_ref)
        load_m = copies.start(m_hbm.at[rank], m_ref)
        load_v = copies.start(v_hbm.at[rank], v_ref)
        load_q = copies.start(mq_hbm.at[rank], mq_ref)

        def bring(member, carry):
            scale = decode_scale(pay_ref, (member,), rows, panels)
            at = pl.multiple_of(member * rows, rows)
            for p in range(panels):
                part = decode(pay_ref, (member,), rows, p, scale)
                g_ref[pl.ds(at, rows), pl.ds(p * LANES, LANES)] = part
                high, low = split(part)
                for n, piece in enumerate((high, low, high)):
                    bs_ref[pl.ds(n * width + at, rows), pl.ds(p * LANES, LANES)] = piece
            return carry

        lax.fori_loop(0, members, bring, 0)
        stores = [copies.start(g_ref, g_hbm)]
        load_l.wait()
        put_cols(qlt_ref, slice(None), ql_ref[...].T, LEFT)
        for t in tiles(width):
            put_cols(as_ref, t, dot_nn(qlt_ref[t, :], bs_ref[...]), LEFT)
        load_r.wait()
        put_rows(qrs_ref, 0, width, qr_ref[...])
        load_v.wait()
        load_q.wait()
        for t in tiles(width):
            rot = dot_nn(as_ref[t, :], qrs_ref[...])
            second = BETA_TWO * v_ref[t, :] + (1.0 - BETA_TWO) * rot * rot
            v_ref[t, :] = second
            first = BETA_ONE * mq_ref[t, :] + (1.0 - BETA_ONE) * rot
            put_rows(bn_ref, t.start, width, first / (jnp.sqrt(second) + 1e-08))
        stores.append(copies.start(v_ref, v1_hbm.at[rank]))
        put_cols(ql3_ref, slice(None), ql_ref[...], LEFT)
        for t in tiles(width):
            put_cols(ab_ref, t, dot_nn(ql3_ref[t, :], bn_ref[...]), LEFT)
        put_cols(qrp_ref, slice(None), qr_ref[...], (0, 1, 0))
        depth = (place_ref[2] - 1 - depth_ref[base + place_ref[1]]).astype(F32)
        factor = jnp.exp(SHRINK * jnp.full((1, width), depth, F32))
        for t in tiles(width):
            u_ref[t, :] = (factor * dot_nt(ab_ref[t, :], qrp_ref[...])).astype(BF16)
        stores.append(copies.start(u_ref, u_hbm))
        load_m.wait()
        m_ref[...] = BETA_ONE * m_ref[...] + (1.0 - BETA_ONE) * g_ref[...]
        stores.append(copies.start(m_ref, m1_hbm.at[rank]))
        for store in stores:
            store.wait()


def update_call(rank, info, pay, ql, qr, m, v, mq, carried):
    width = ql.shape[1]
    state = jax.ShapeDtypeStruct(m.shape, F32)
    flat = pltpu.VMEM((width, width), F32)
    wide = pltpu.VMEM((width, 3 * width), BF16)
    tall = pltpu.VMEM((3 * width, width), BF16)
    return pl.pallas_call(
        functools.partial(update_kernel, rank, rank * info[1].shape[0]),
        grid=(1,),
        out_shape=(
            jax.ShapeDtypeStruct((width, width), F32),
            jax.ShapeDtypeStruct((width, width), BF16),
            state,
            state,
        ),
        in_specs=[SMEM] * 3 + [pl.BlockSpec(pay.shape, lambda *_: (0, 0, 0))] + [ANY] * (5 + len(carried)),
        out_specs=(ANY,) * 4,
        scratch_shapes=[flat, pltpu.VMEM((width, width), BF16)]
        + [flat] * 5
        + [wide, wide, tall, wide, tall, tall, wide, wide, pltpu.SemaphoreType.DMA((9,))],
        input_output_aliases={9: 2, 10: 3} if carried else {},
        compiler_params=params(),
        cost_estimate=cost(4 * 3 * 2 * width**3, 10 * 4 * width**2),
        name="update",
    )(*info, pay, ql, qr, m, v, mq, *carried)


def basis_kernel(rank, left, place_ref, count_ref, g_hbm, s_hbm, q_hbm, *refs):
    s1_hbm, q1_hbm, g_ref, s_ref, q_ref, y_ref, cols_ref, a_ref, b_ref, sems = refs[-10:]
    width = g_ref.shape[0]
    live = count_ref[place_ref[1]] > rank
    near, far, one = pl.ds(0, 3 * width), pl.ds(width, 3 * width), pl.ds(0, width)

    @pl.when(jnp.logical_not(live))
    def _():
        copies = Copies(sems)
        loads = [copies.start(s_hbm.at[rank], s_ref), copies.start(q_hbm.at[rank], q_ref)]
        stores = []
        for load, ref, out in zip(loads, (s_ref, q_ref), (s1_hbm, q1_hbm)):
            load.wait()
            stores.append(copies.start(ref, out.at[rank]))
        for store in stores:
            store.wait()

    @pl.when(live)
    def _():
        copies = Copies(sems)
        load_g = copies.start(g_hbm, g_ref)
        load_q = copies.start(q_hbm.at[rank], q_ref)
        load_s = copies.start(s_hbm.at[rank], s_ref)
        load_g.wait()
        put_cols(cols_ref, slice(None), g_ref[...] if left else g_ref[...].T, BOTH)
        load_q.wait()
        put_cols(a_ref, slice(None), q_ref[...].T, LEFT)
        load_s.wait()
        for t in tiles(width):
            outer = dot_nt(cols_ref[t, near], cols_ref[:, far])
            stat = BETA_TWO * s_ref[t, :] + (1.0 - BETA_TWO) * outer
            s_ref[t, :] = stat
            put_rows(b_ref, t.start, width, stat)
        stores = [copies.start(s_ref, s1_hbm.at[rank])]
        turned = dot_nn(a_ref[...], b_ref[...])
        squares = jnp.sum(turned * turned, axis=0, keepdims=True)
        mean = jnp.sum(squares, axis=1, keepdims=True) * (1.0 / (width * width))
        y_ref[...] = turned * (0.4 / (math.sqrt(width) * jnp.sqrt(mean + 1e-06)))

        def step(i, carry):
            put_cols(cols_ref, slice(None), y_ref[...], BOTH)
            put_rows(b_ref, 0, width, y_ref[...])
            put_cols(a_ref, slice(None), dot_nt(cols_ref[:, near], cols_ref[:, far]), LEFT)
            y_ref[...] = 1.5 * y_ref[...] - 0.5 * dot_nn(a_ref[...], b_ref[...])
            return carry

        high = y_ref[...].astype(BF16)
        cols_ref[:, one] = high
        b_ref[one, :] = high
        a_ref[:, one] = dot_nt(cols_ref[:, one], cols_ref[:, one]).astype(BF16)
        y_ref[...] = 1.5 * y_ref[...] - 0.5 * dot_nn(a_ref[:, one], b_ref[one, :])
        lax.fori_loop(1, ITERS, step, 0)
        q_ref[...] = y_ref[...].T
        stores.append(copies.start(q_ref, q1_hbm.at[rank]))
        for store in stores:
            store.wait()


def basis_call(rank, left, info, grad, stat, basis, carried, after=()):
    width = grad.shape[0]
    state = jax.ShapeDtypeStruct(stat.shape, F32)
    flat = pltpu.VMEM((width, width), F32)
    return pl.pallas_call(
        functools.partial(basis_kernel, rank, left),
        out_shape=(state, state),
        in_specs=[SMEM, SMEM] + [ANY] * (3 + len(carried) + len(after)),
        out_specs=(ANY, ANY),
        scratch_shapes=[flat] * 4
        + [
            pltpu.VMEM((width, 4 * width), BF16),
            pltpu.VMEM((width, 3 * width), BF16),
            pltpu.VMEM((3 * width, width), BF16),
            pltpu.SemaphoreType.DMA((5,)),
        ],
        input_output_aliases={5: 0, 6: 1} if carried else {},
        compiler_params=params(),
        cost_estimate=cost((2 + 2 * ITERS) * 3 * 2 * width**3, 5 * 4 * width**2),
        name="basis_left" if left else "basis_right",
    )(*info[:2], grad, stat, basis, *carried, *after)


def pick_kernel(groups, members, count, place_ref, owner_ref, rank_ref, *refs):
    sources, out_ref, sems = refs[:-2], refs[-2], refs[-1]

    def start(i, carry):
        block = place_ref[0] * count + i
        owner = owner_ref[block]
        which = rank_ref[block] * groups + ((owner // members) ^ place_ref[0])
        for n, source in enumerate(sources):

            @pl.when(which == n)
            def _():
                pltpu.make_async_copy(source.at[owner % members], out_ref.at[i], sems.at[i]).start()

        return carry

    def wait(i, carry):
        pltpu.make_async_copy(sources[0].at[0], out_ref.at[i], sems.at[i]).wait()
        return carry

    lax.fori_loop(0, count, start, 0)
    lax.fori_loop(0, count, wait, 0)


def pick(place, owner_device, rank_of, sources, groups, members):
    rows, width = sources[0].shape[1:]
    count = owner_device.shape[0] // groups
    return pl.pallas_call(
        functools.partial(pick_kernel, groups, members, count),
        out_shape=jax.ShapeDtypeStruct((count, rows, width), BF16),
        in_specs=[SMEM] * 3 + [ANY] * len(sources),
        out_specs=pl.BlockSpec(memory_space=pltpu.VMEM),
        scratch_shapes=[pltpu.SemaphoreType.DMA((count,))],
        compiler_params=params(ROOMY),
        cost_estimate=cost(0, 4 * count * rows * width),
        name="pick",
    )(place, owner_device, rank_of, *sources)


def local(
    partial_grads,
    owner_device,
    layer_of,
    stat_left,
    stat_right,
    basis_left,
    basis_right,
    moment_first,
    moment_second,
):
    capacity = stat_left.shape[0]
    width = stat_left.shape[1]
    groups = lax.axis_size("dp")
    members = lax.axis_size("mp")
    halves = groups // 2
    grads = partial_grads[0]
    rows = grads.shape[1]
    own = lax.axis_index(("dp", "mp"))
    place = jnp.stack([lax.axis_index("dp"), own, groups])

    def flip(x, bits):
        return lax.ppermute(x, "dp", [(i, i ^ bits) for i in range(groups)])

    block_at, rank_of, counts, layer_at, packed = route(
        owner_device, layer_of, place, grads, capacity, halves, members
    )
    info = (place, counts, layer_at)
    from_core = [flip(packed, 1)]
    for k in range(1, capacity):
        from_core.append(flip(pack(k, place, block_at, grads, halves, members), 1))

    from_x = [[] for _ in range(capacity)]
    step = halves // 2
    mixed, after = None, ()
    while step:
        for k in range(capacity):
            sent, mark = fold(k, step, step, place, block_at, grads, from_core[k], from_x[k], members, after)
            from_x[k].append(flip(sent, 2 * step))
            if mixed is None:
                mixed, mark = premix(place, counts, basis_left, basis_right, moment_first, (mark,))
            after = (mark,)
        step //= 2

    arrived = []
    for k in range(capacity):
        ready, mark = fold(k, 0, 1, place, block_at, grads, from_core[k], from_x[k], members, after)
        after = (mark,)
        arrived.append(lax.all_to_all(ready[0], "mp", split_axis=0, concat_axis=0, tiled=True))

    sources, gradients, moments, returned, crossed = [], [], (), [], []
    for k in range(capacity):
        grad, block_update, *moments = update_call(
            k, info, arrived[k], basis_left, basis_right, moment_first, moment_second, mixed, tuple(moments)
        )
        gradients.append(grad)
        pieces = lax.all_to_all(
            block_update.reshape(members, rows, width), "mp", split_axis=0, concat_axis=0, tiled=True
        )
        held = [pieces]
        step = 1
        while step < halves:
            held = held + [flip(part, 2 * step) for part in held]
            step *= 2
        returned.append(pieces)
        crossed.append(held[-1])
        for part in held:
            sources += [part, flip(part, 1)]

    lefts, rights = (), ()
    waits = [(), (returned[-1],)] + [(returned[-1],)] * (2 * capacity - 3) + [(crossed[-1],)]
    for k in range(capacity):
        rights = basis_call(k, False, info, gradients[k], stat_right, basis_right, tuple(rights), waits[2 * k])
        lefts = basis_call(k, True, info, gradients[k], stat_left, basis_left, tuple(lefts), waits[2 * k + 1])

    update_rows = pick(place, owner_device, rank_of, sources, groups, members)
    return (update_rows, lefts[0], rights[0], lefts[1], rights[1], moments[0], moments[1])


def solution(mesh):
    slots = P(("dp", "mp"), None, None)
    in_specs = (P("dp", None, "mp", None), P(), P()) + (slots,) * 6
    out_specs = (P("dp", "mp", None),) + (slots,) * 6
    return jax.shard_map(local, mesh=mesh, in_specs=in_specs, out_specs=out_specs, check_vma=False)
```

```python
import functools
import math

import jax
import jax.numpy as jnp
from jax import lax
from jax.experimental import pallas as pl
from jax.experimental.pallas import tpu as pltpu
from jax.sharding import PartitionSpec as P

ITERS = 4
BETA_ONE = 0.9
BETA_TWO = 0.95
SHRINK = math.log(0.8)
LANES = 128
TAIL = 16
MIB = 1 << 20
ROOMY = 24 * MIB
WEIGHT = 1.0
LATE = 8
F32 = jnp.float32
BF16 = jnp.bfloat16
ANY = pl.BlockSpec(memory_space=pl.ANY)
SMEM = pl.BlockSpec(memory_space=pltpu.SMEM)


def params(limit=60 * MIB):
    return pltpu.CompilerParams(vmem_limit_bytes=limit)


def cost(flops, moved):
    return pl.CostEstimate(flops=int(flops * WEIGHT), bytes_accessed=int(moved * WEIGHT), transcendentals=0)


def gather(base, halves, members, place_ref, block_ref, grads_ref, out_ref, sems):
    copies = []
    for i in range(halves * members):
        group = place_ref[0] ^ (2 * (i // members) + 1)
        block = block_ref[base + group * members + i % members]
        copies.append(
            pltpu.make_async_copy(grads_ref.at[block], out_ref.at[i // members, i % members], sems.at[i])
        )
        copies[-1].start()
    for copy in copies:
        copy.wait()


def route_kernel(
    capacity, halves, members, owner_ref, layer_ref, place_ref, grads_ref,
    block_ref, rank_ref, count_ref, depth_ref, out_ref, sems,
):
    devices = 2 * halves * members
    for d in range(devices):
        count_ref[d] = 0
        for k in range(capacity):
            block_ref[k * devices + d] = 0
            depth_ref[k * devices + d] = 0
    for b in range(owner_ref.shape[0]):
        owner = owner_ref[b]
        rank = count_ref[owner]
        rank_ref[b] = rank
        block_ref[rank * devices + owner] = b
        depth_ref[rank * devices + owner] = layer_ref[b]
        count_ref[owner] = rank + 1
    gather(0, halves, members, place_ref, block_ref, grads_ref, out_ref, sems)


def route(owner_device, layer_of, place, grads, capacity, halves, members):
    devices = 2 * halves * members
    packed = (halves, members) + grads.shape[1:]
    flat = jax.ShapeDtypeStruct((capacity * devices,), jnp.int32)
    return pl.pallas_call(
        functools.partial(route_kernel, capacity, halves, members),
        out_shape=(
            flat,
            jax.ShapeDtypeStruct(owner_device.shape, jnp.int32),
            jax.ShapeDtypeStruct((devices,), jnp.int32),
            flat,
            jax.ShapeDtypeStruct(packed, grads.dtype),
        ),
        in_specs=[SMEM, SMEM, SMEM, ANY],
        out_specs=(SMEM,) * 4 + (pl.BlockSpec(memory_space=pltpu.VMEM),),
        scratch_shapes=[pltpu.SemaphoreType.DMA((halves * members,))],
        compiler_params=params(),
        cost_estimate=cost(0, 4 * math.prod(packed)),
        name="route",
    )(owner_device, layer_of, place, grads)


def pack(rank, place, block_at, grads, halves, members):
    packed = (halves, members) + grads.shape[1:]
    return pl.pallas_call(
        functools.partial(gather, rank * 2 * halves * members, halves, members),
        out_shape=jax.ShapeDtypeStruct(packed, grads.dtype),
        in_specs=[SMEM, SMEM, ANY],
        out_specs=pl.BlockSpec(memory_space=pltpu.VMEM),
        scratch_shapes=[pltpu.SemaphoreType.DMA((halves * members,))],
        compiler_params=params(),
        cost_estimate=cost(0, 4 * math.prod(packed)),
        name="pack",
    )(place, block_at, grads)


def decode_scale(ref, lead, rows, panels):
    tail = ref[lead + (pl.ds(panels * rows, TAIL), slice(None))].astype(jnp.int32).astype(F32)
    power = jnp.concatenate([tail] * (LANES // TAIL), axis=0).T
    return jnp.exp2(-power[:rows])


def decode(ref, lead, rows, panel, scale):
    part = ref[lead + (pl.ds(panel * rows, rows), slice(None))]
    return part.astype(jnp.int32).astype(F32) * scale


def fold_kernel(base, first, members, earlier_count, place_ref, block_ref, grads_ref, core_ref, *refs):
    earlier, (out_ref, done_ref, raw_ref, sems) = refs[:earlier_count], refs[-4:]
    done_ref[0] = 1
    count = out_ref.shape[0]
    rows, width = raw_ref.shape[1:]
    panels = width // LANES
    for i in range(count * members):
        group = place_ref[0] ^ (2 * (first + i // members))
        block = block_ref[base + group * members + i % members]
        pltpu.make_async_copy(grads_ref.at[block], raw_ref.at[i], sems.at[i]).start()

    def piece(i, carry):
        pltpu.make_async_copy(grads_ref.at[0], raw_ref.at[i], sems.at[i]).wait()
        at = (i // members, i % members)
        total = raw_ref[i].astype(F32) + core_ref[at].astype(F32)
        parts = [total[:, p * LANES : (p + 1) * LANES] for p in range(panels)]
        for ref in earlier:
            scale = decode_scale(ref, at, rows, panels)
            parts = [part + decode(ref, at, rows, p, scale) for p, part in enumerate(parts)]
        largest = functools.reduce(jnp.maximum, [jnp.abs(part) for part in parts])
        largest = jnp.max(largest, axis=1, keepdims=True)
        power = jnp.floor(14.99 - jnp.log2(jnp.maximum(largest, 1e-26)))
        wide = jnp.broadcast_to(power, (rows, LANES))
        scale = jnp.exp2(wide)
        for p, part in enumerate(parts):
            out_ref[at + (pl.ds(p * rows, rows), slice(None))] = (
                jnp.round(part * scale).astype(jnp.int32).astype(jnp.int16)
            )
        if rows < LANES:
            wide = jnp.concatenate([wide, jnp.zeros((LANES - rows, LANES), F32)], axis=0)
        out_ref[at + (pl.ds(panels * rows, TAIL), slice(None))] = (
            wide.T[:TAIL].astype(jnp.int32).astype(jnp.int16)
        )
        return carry

    lax.fori_loop(0, count * members, piece, 0)


def fold(rank, first, count, place, block_at, grads, from_core, from_x, members, after=(), weight=8):
    rows, width = grads.shape[1:]
    tall = (width // LANES) * rows + TAIL
    devices = 2 * from_core.shape[0] * members
    at = first // count
    return pl.pallas_call(
        functools.partial(fold_kernel, rank * devices, first, members, len(from_x)),
        grid=(1,),
        in_specs=[SMEM, SMEM, ANY, pl.BlockSpec((count, members, rows, width), lambda i: (at, 0, 0, 0))]
        + [pl.BlockSpec((count, members, tall, LANES), lambda i: (at, 0, 0, 0)) for _ in from_x]
        + [SMEM] * len(after),
        out_specs=(pl.BlockSpec((count, members, tall, LANES), lambda i: (0, 0, 0, 0)), SMEM),
        out_shape=(
            jax.ShapeDtypeStruct((count, members, tall, LANES), jnp.int16),
            jax.ShapeDtypeStruct((1,), jnp.int32),
        ),
        scratch_shapes=[
            pltpu.VMEM((count * members, rows, width), grads.dtype),
            pltpu.SemaphoreType.DMA((count * members,)),
        ],
        compiler_params=params(ROOMY),
        cost_estimate=cost(0, weight * count * members * rows * width),
        name="fold",
    )(place, block_at, grads, from_core, *from_x, *after)


def split(x):
    high = x.astype(BF16)
    return high, (x - high.astype(F32)).astype(BF16)


def put_cols(ref, rows, x, order):
    width = x.shape[1]
    pieces = split(x)
    for n, which in enumerate(order):
        ref[rows, pl.ds(n * width, width)] = pieces[which]


def put_rows(ref, start, height, x):
    high, low = split(x)
    size = x.shape[0]
    ref[pl.ds(start, size), :] = high
    ref[pl.ds(height + start, size), :] = low
    ref[pl.ds(2 * height + start, size), :] = high


def dot_nn(a, b):
    return lax.dot_general(a, b, (((1,), (0,)), ((), ())), preferred_element_type=F32)


def dot_nt(a, b):
    return lax.dot_general(a, b, (((1,), (1,)), ((), ())), preferred_element_type=F32)


LEFT = (0, 0, 1)
BOTH = (0, 0, 1, 0)


def tiles(height, size=512):
    return [pl.ds(s, size) for s in range(0, height, size)]


class Copies:
    def __init__(self, sems):
        self.sems, self.used = sems, 0

    def start(self, source, target):
        copy = pltpu.make_async_copy(source, target, self.sems.at[self.used])
        self.used += 1
        copy.start()
        return copy


def premix_kernel(slots, place_ref, count_ref, ql_hbm, qr_hbm, m_hbm, *refs):
    mq_hbm, done_ref, ql_ref, qr_ref, m_ref, qlt_ref, b_ref, a_ref, sems = refs[-9:]
    width = ql_ref.shape[0]
    done_ref[0] = 1
    for slot in range(slots):

        @pl.when(count_ref[place_ref[1]] > slot)
        def _():
            copies = Copies(sems)
            load_m = copies.start(m_hbm.at[slot], m_ref)
            load_l = copies.start(ql_hbm.at[slot], ql_ref)
            load_r = copies.start(qr_hbm.at[slot], qr_ref)
            load_m.wait()
            put_rows(b_ref, 0, width, m_ref[...])
            load_l.wait()
            put_cols(qlt_ref, slice(None), ql_ref[...].T, LEFT)
            for t in tiles(width):
                put_cols(a_ref, t, dot_nn(qlt_ref[t, :], b_ref[...]), LEFT)
            load_r.wait()
            put_rows(b_ref, 0, width, qr_ref[...])
            for t in tiles(width):
                m_ref[t, :] = dot_nn(a_ref[t, :], b_ref[...])
            copies.start(m_ref, mq_hbm.at[slot]).wait()


def premix(place, counts, ql, qr, m, after):
    slots, width = ql.shape[:2]
    flat = pltpu.VMEM((width, width), F32)
    wide = pltpu.VMEM((width, 3 * width), BF16)
    tall = pltpu.VMEM((3 * width, width), BF16)
    return pl.pallas_call(
        functools.partial(premix_kernel, slots),
        out_shape=(jax.ShapeDtypeStruct(m.shape, F32), jax.ShapeDtypeStruct((1,), jnp.int32)),
        in_specs=[SMEM, SMEM] + [ANY] * 3 + [SMEM] * len(after),
        out_specs=(ANY, SMEM),
        scratch_shapes=[flat, flat, flat, wide, tall, wide, pltpu.SemaphoreType.DMA((4,))],
        compiler_params=params(),
        cost_estimate=cost(slots * 2 * 3 * 2 * width**3, slots * 4 * 4 * width**2),
        name="premix",
    )(place, counts, ql, qr, m, *after)


def update_kernel(rank, base, place_ref, count_ref, depth_ref, pay_ref, ql_hbm, qr_hbm, m_hbm, v_hbm, mq_hbm, *refs):
    g_hbm, u_hbm, m1_hbm, v1_hbm = refs[-20:-16]
    g_ref, u_ref, ql_ref, qr_ref, m_ref, v_ref, mq_ref, qlt_ref, ql3_ref, qrs_ref, qrp_ref, bs_ref, bn_ref, as_ref, ab_ref, sems = refs[-16:]
    width = g_ref.shape[0]
    members = pay_ref.shape[0]
    rows = width // members
    panels = width // LANES
    live = count_ref[place_ref[1]] > rank

    @pl.when(jnp.logical_not(live))
    def _():
        copies = Copies(sems)
        loads = [copies.start(m_hbm.at[rank], m_ref), copies.start(v_hbm.at[rank], v_ref)]
        u_ref[...] = jnp.zeros_like(u_ref)
        stores = [copies.start(u_ref, u_hbm.at[:, rank])]
        for load in loads:
            load.wait()
        stores += [copies.start(m_ref, m1_hbm.at[rank]), copies.start(v_ref, v1_hbm.at[rank])]
        for store in stores:
            store.wait()

    @pl.when(live)
    def _():
        copies = Copies(sems)
        load_l = copies.start(ql_hbm.at[rank], ql_ref)
        load_r = copies.start(qr_hbm.at[rank], qr_ref)
        load_m = copies.start(m_hbm.at[rank], m_ref)
        load_v = copies.start(v_hbm.at[rank], v_ref)
        load_q = copies.start(mq_hbm.at[rank], mq_ref)

        def bring(member, carry):
            scale = decode_scale(pay_ref, (member,), rows, panels)
            at = pl.multiple_of(member * rows, rows)
            for p in range(panels):
                part = decode(pay_ref, (member,), rows, p, scale)
                g_ref[pl.ds(at, rows), pl.ds(p * LANES, LANES)] = part
                high, low = split(part)
                for n, piece in enumerate((high, low, high)):
                    bs_ref[pl.ds(n * width + at, rows), pl.ds(p * LANES, LANES)] = piece
            return carry

        lax.fori_loop(0, members, bring, 0)
        stores = [copies.start(g_ref, g_hbm)]
        load_l.wait()
        put_cols(qlt_ref, slice(None), ql_ref[...].T, LEFT)
        for t in tiles(width):
            put_cols(as_ref, t, dot_nn(qlt_ref[t, :], bs_ref[...]), LEFT)
        load_r.wait()
        put_rows(qrs_ref, 0, width, qr_ref[...])
        load_v.wait()
        load_q.wait()
        for t in tiles(width):
            rot = dot_nn(as_ref[t, :], qrs_ref[...])
            second = BETA_TWO * v_ref[t, :] + (1.0 - BETA_TWO) * rot * rot
            v_ref[t, :] = second
            first = BETA_ONE * mq_ref[t, :] + (1.0 - BETA_ONE) * rot
            put_rows(bn_ref, t.start, width, first / (jnp.sqrt(second) + 1e-08))
        stores.append(copies.start(v_ref, v1_hbm.at[rank]))
        put_cols(ql3_ref, slice(None), ql_ref[...], LEFT)
        for t in tiles(width):
            put_cols(ab_ref, t, dot_nn(ql3_ref[t, :], bn_ref[...]), LEFT)
        put_cols(qrp_ref, slice(None), qr_ref[...], (0, 1, 0))
        depth = (place_ref[2] - 1 - depth_ref[base + place_ref[1]]).astype(F32)
        factor = jnp.exp(SHRINK * jnp.full((1, width), depth, F32))
        direction = (factor * dot_nt(ab_ref[...], qrp_ref[...])).astype(BF16)
        u_ref[...] = direction.reshape(members, rows, width)
        stores.append(copies.start(u_ref, u_hbm.at[:, rank]))
        load_m.wait()
        m_ref[...] = BETA_ONE * m_ref[...] + (1.0 - BETA_ONE) * g_ref[...]
        stores.append(copies.start(m_ref, m1_hbm.at[rank]))
        for store in stores:
            store.wait()


def update_call(rank, info, pay, ql, qr, m, v, mq, carried):
    slots, width = ql.shape[:2]
    members = pay.shape[0]
    state = jax.ShapeDtypeStruct(m.shape, F32)
    flat = pltpu.VMEM((width, width), F32)
    wide = pltpu.VMEM((width, 3 * width), BF16)
    tall = pltpu.VMEM((3 * width, width), BF16)
    return pl.pallas_call(
        functools.partial(update_kernel, rank, rank * info[1].shape[0]),
        grid=(1,),
        out_shape=(
            jax.ShapeDtypeStruct((width, width), F32),
            jax.ShapeDtypeStruct((members, slots, width // members, width), BF16),
            state,
            state,
        ),
        in_specs=[SMEM] * 3 + [pl.BlockSpec(pay.shape, lambda *_: (0, 0, 0))] + [ANY] * (5 + len(carried)),
        out_specs=(ANY,) * 4,
        scratch_shapes=[flat, pltpu.VMEM((members, width // members, width), BF16)]
        + [flat] * 5
        + [wide, wide, tall, wide, tall, tall, wide, wide, pltpu.SemaphoreType.DMA((9,))],
        input_output_aliases={9: 1, 10: 2, 11: 3} if carried else {},
        compiler_params=params(),
        cost_estimate=cost(4 * 3 * 2 * width**3, 10 * 4 * width**2),
        name="update",
    )(*info, pay, ql, qr, m, v, mq, *carried)


def basis_kernel(rank, left, place_ref, count_ref, g_hbm, s_hbm, q_hbm, *refs):
    s1_hbm, q1_hbm, done_ref, g_ref, s_ref, q_ref, y_ref, cols_ref, a_ref, b_ref, sems = refs[-11:]
    done_ref[0] = 1
    width = g_ref.shape[0]
    live = count_ref[place_ref[1]] > rank
    near, far, one = pl.ds(0, 3 * width), pl.ds(width, 3 * width), pl.ds(0, width)

    @pl.when(jnp.logical_not(live))
    def _():
        copies = Copies(sems)
        loads = [copies.start(s_hbm.at[rank], s_ref), copies.start(q_hbm.at[rank], q_ref)]
        stores = []
        for load, ref, out in zip(loads, (s_ref, q_ref), (s1_hbm, q1_hbm)):
            load.wait()
            stores.append(copies.start(ref, out.at[rank]))
        for store in stores:
            store.wait()

    @pl.when(live)
    def _():
        copies = Copies(sems)
        load_g = copies.start(g_hbm, g_ref)
        load_q = copies.start(q_hbm.at[rank], q_ref)
        load_s = copies.start(s_hbm.at[rank], s_ref)
        load_g.wait()
        put_cols(cols_ref, slice(None), g_ref[...] if left else g_ref[...].T, BOTH)
        load_q.wait()
        put_cols(a_ref, slice(None), q_ref[...].T, LEFT)
        load_s.wait()
        for t in tiles(width):
            outer = dot_nt(cols_ref[t, near], cols_ref[:, far])
            stat = BETA_TWO * s_ref[t, :] + (1.0 - BETA_TWO) * outer
            s_ref[t, :] = stat
            put_rows(b_ref, t.start, width, stat)
        stores = [copies.start(s_ref, s1_hbm.at[rank])]
        turned = dot_nn(a_ref[...], b_ref[...])
        squares = jnp.sum(turned * turned, axis=0, keepdims=True)
        mean = jnp.sum(squares, axis=1, keepdims=True) * (1.0 / (width * width))
        y_ref[...] = turned * (0.4 / (math.sqrt(width) * jnp.sqrt(mean + 1e-06)))

        def step(i, carry):
            put_cols(cols_ref, slice(None), y_ref[...], BOTH)
            put_rows(b_ref, 0, width, y_ref[...])
            put_cols(a_ref, slice(None), dot_nt(cols_ref[:, near], cols_ref[:, far]), LEFT)
            y_ref[...] = 1.5 * y_ref[...] - 0.5 * dot_nn(a_ref[...], b_ref[...])
            return carry

        high = y_ref[...].astype(BF16)
        cols_ref[:, one] = high
        b_ref[one, :] = high
        a_ref[:, one] = dot_nt(cols_ref[:, one], cols_ref[:, one]).astype(BF16)
        y_ref[...] = 1.5 * y_ref[...] - 0.5 * dot_nn(a_ref[:, one], b_ref[one, :])
        lax.fori_loop(1, ITERS, step, 0)
        q_ref[...] = y_ref[...].T
        stores.append(copies.start(q_ref, q1_hbm.at[rank]))
        for store in stores:
            store.wait()


def basis_call(rank, left, info, grad, stat, basis, carried, after=()):
    width = grad.shape[0]
    state = jax.ShapeDtypeStruct(stat.shape, F32)
    flat = pltpu.VMEM((width, width), F32)
    return pl.pallas_call(
        functools.partial(basis_kernel, rank, left),
        out_shape=(state, state, jax.ShapeDtypeStruct((1,), jnp.int32)),
        in_specs=[SMEM, SMEM] + [ANY] * (3 + len(carried)) + [SMEM] * len(after),
        out_specs=(ANY, ANY, SMEM),
        scratch_shapes=[flat] * 4
        + [
            pltpu.VMEM((width, 4 * width), BF16),
            pltpu.VMEM((width, 3 * width), BF16),
            pltpu.VMEM((3 * width, width), BF16),
            pltpu.SemaphoreType.DMA((5,)),
        ],
        input_output_aliases={5: 0, 6: 1} if carried else {},
        compiler_params=params(),
        cost_estimate=cost((2 + 2 * ITERS) * 3 * 2 * width**3, 5 * 4 * width**2),
        name="basis_left" if left else "basis_right",
    )(*info[:2], grad, stat, basis, *carried, *after)


def pick_kernel(members, count, place_ref, owner_ref, rank_ref, after_ref, *refs):
    sources, out_ref, sems = refs[:-2], refs[-2], refs[-1]

    def start(i, carry):
        block = place_ref[0] * count + i
        owner = owner_ref[block]
        which = (owner // members) ^ place_ref[0]
        for n, source in enumerate(sources):

            @pl.when(which == n)
            def _():
                pltpu.make_async_copy(source.at[owner % members, rank_ref[block]], out_ref.at[i], sems.at[i]).start()

        return carry

    def wait(i, carry):
        pltpu.make_async_copy(sources[0].at[0, 0], out_ref.at[i], sems.at[i]).wait()
        return carry

    lax.fori_loop(0, count, start, 0)
    lax.fori_loop(0, count, wait, 0)


def pick(place, owner_device, rank_of, sources, groups, members, after):
    rows, width = sources[0].shape[2:]
    count = owner_device.shape[0] // groups
    return pl.pallas_call(
        functools.partial(pick_kernel, members, count),
        out_shape=jax.ShapeDtypeStruct((count, rows, width), BF16),
        in_specs=[SMEM] * 4 + [ANY] * len(sources),
        out_specs=pl.BlockSpec(memory_space=pltpu.VMEM),
        scratch_shapes=[pltpu.SemaphoreType.DMA((count,))],
        compiler_params=params(ROOMY),
        cost_estimate=cost(0, 4 * count * rows * width),
        name="pick",
    )(place, owner_device, rank_of, after, *sources)


def local(
    partial_grads,
    owner_device,
    layer_of,
    stat_left,
    stat_right,
    basis_left,
    basis_right,
    moment_first,
    moment_second,
):
    capacity = stat_left.shape[0]
    width = stat_left.shape[1]
    groups = lax.axis_size("dp")
    members = lax.axis_size("mp")
    halves = groups // 2
    grads = partial_grads[0]
    rows = grads.shape[1]
    own = lax.axis_index(("dp", "mp"))
    place = jnp.stack([lax.axis_index("dp"), own, groups])

    def flip(x, bits):
        return lax.ppermute(x, "dp", [(i, i ^ bits) for i in range(groups)])

    block_at, rank_of, counts, layer_at, packed = route(
        owner_device, layer_of, place, grads, capacity, halves, members
    )
    info = (place, counts, layer_at)
    from_core = [flip(packed, 1)]
    for k in range(1, capacity):
        from_core.append(flip(pack(k, place, block_at, grads, halves, members), 1))

    from_x = [[] for _ in range(capacity)]
    step = halves // 2
    mixed, after = None, ()
    while step:
        for k in range(capacity):
            sent, mark = fold(k, step, step, place, block_at, grads, from_core[k], from_x[k], members, after)
            from_x[k].append(flip(sent, 2 * step))
            if mixed is None:
                mixed, mark = premix(place, counts, basis_left, basis_right, moment_first, (mark,))
            after = (mark,)
        step //= 2

    arrived = []
    for k in range(capacity):
        ready, mark = fold(k, 0, 1, place, block_at, grads, from_core[k], from_x[k], members, after, LATE if k else 8)
        after = (mark,)
        arrived.append(lax.all_to_all(ready[0], "mp", split_axis=0, concat_axis=0, tiled=True))

    gradients, carried = [], ()
    for k in range(capacity):
        grad, *carried = update_call(
            k, info, arrived[k], basis_left, basis_right, moment_first, moment_second, mixed, tuple(carried)
        )
        gradients.append(grad)
    block_updates, *moments = carried
    returned = lax.all_to_all(block_updates, "mp", split_axis=0, concat_axis=0, tiled=True)
    lefts, rights, after = (), (), ()
    for k in range(capacity):
        *rights, mark = basis_call(k, False, info, gradients[k], stat_right, basis_right, tuple(rights), after)
        *lefts, mark = basis_call(k, True, info, gradients[k], stat_left, basis_left, tuple(lefts), (mark,))
        if k == 0:
            returned, mark = lax.optimization_barrier((returned, mark))
            after = (mark,)
            held = [returned]
            step = 1
            while step < halves:
                held = held + [flip(part, 2 * step) for part in held]
                step *= 2
    *far, mark = lax.optimization_barrier((*held[1:], mark))
    sources = []
    for part in held[:1] + far:
        sources += [part, flip(part, 1)]

    update_rows = pick(place, owner_device, rank_of, sources, groups, members, mark)
    return (update_rows, lefts[0], rights[0], lefts[1], rights[1], moments[0], moments[1])


def solution(mesh):
    slots = P(("dp", "mp"), None, None)
    in_specs = (P("dp", None, "mp", None), P(), P()) + (slots,) * 6
    out_specs = (P("dp", "mp", None),) + (slots,) * 6
    return jax.shard_map(local, mesh=mesh, in_specs=in_specs, out_specs=out_specs, check_vma=False)
```
